256 devices in a mesh: gz: 128 (over x, z_hi, y, core), ga: 2 (over z_lo).
Axes of the slice: x: 4, y: 4, z: 8 (z_hi: 4, z_lo: 2; z = z_hi * 2 + z_lo), core: 2. Of those that a mesh axis runs over, the one named last changes fastest.
Arguments:
- fractions: float32 [16, 512, 128, 128], P('ga', 'gz'), may hold values from 0.05 to 1
- courant: float32 [16], replicated, may hold values from -0.9 to 0.9, as said below
- spread: float32 [16], replicated, may hold values from 0.05 to 0.25
- inlet_frac: float32 [16], replicated, may hold values from 0.2 to 1
- flags: int32 [512, 128, 128], P('gz'), may hold values from 0 to 7
- table_index: int32 [512, 128], P('gz'), may hold values from 0 to 31
- lin_table: float32 [32, 16, 16], replicated, may hold values from -1.5 to 1.5
- quad_table: float32 [32, 16, 16], replicated, may hold values from -0.9 to 0.9
Outputs:
- updated: float32 [16, 512, 128, 128], P('ga', 'gz')
The draws below stay inside these ranges and needn't reach their ends.
Inputs may be any that keep to these rules, and one draw needn't show every extreme that they name: Among groups 0 to 7, and in each further run of 8 groups, half have positive and half negative courant; magnitudes lie between 0.3 and 0.9.
All inputs are finite; a program needn't handle non-finite values.
Results may differ from the reference program's by a relative error of at most 0.00007.
Values sent between devices are 32-bit elements; how exact they have to be, the bound alone decides.
No kernel may reach another device: no remote copies, remote signals or barrier semaphores. Data moves between devices by JAX's collectives and lax.ppermute only.
A program may use at most 64 MiB of HBM per device.

```python
import math
import jax
import jax.numpy as jnp
from jax import lax

G = 16
NTAB = 32
BLK = 128
NZT = 512
G_DEV = 8
NBLK = 128


def draw_courant(key, part):
    key_mag = jax.random.fold_in(key, 11)
    key_sign = jax.random.fold_in(key, 23)
    magnitude = jax.random.uniform(key_mag, (G,), jnp.float32, 0.3, 0.9)
    keys = jax.random.split(key_sign, G // G_DEV)
    ranks = jax.vmap(lambda k: jax.random.permutation(k, G_DEV))(keys).reshape(G)
    signs = jnp.where(ranks < G_DEV // 2, 1.0, -1.0).astype(jnp.float32)
    return (magnitude * signs).astype(jnp.float32)


def plant(entries, own_key, least, top_value):
    spot = [jax.random.randint(jax.random.fold_in(own_key, axis), (), 0, length) for axis, length in enumerate(entries.shape)]
    longest = entries.shape.index(max(entries.shape))
    beside = spot[:longest] + [(spot[longest] + 1) % entries.shape[longest]] + spot[longest + 1:]
    return entries.at[tuple(spot)].set(least).at[tuple(beside)].set(top_value)


def block_scale(key, extent, pieces, smallest, top_value):
    def one(position, shards_of):
        steps = jax.random.uniform(jax.random.fold_in(jax.random.fold_in(key, 6), position), (shards_of,), jnp.float32, smallest / len(pieces), top_value / len(pieces))
        return jnp.repeat(jnp.exp(steps), extent[position] // shards_of).reshape((-1,) + (1,) * (len(extent) - position - 1))

    level = one(*pieces[0])
    for cut in pieces[1:]:
        level = level * one(*cut)
    return level


def noise(stream_key, dims, width, limit, dtype=jnp.bfloat16):
    array = width * jax.random.normal(stream_key, dims, jnp.float32)
    return jnp.clip(array, min=-limit, max=limit).astype(dtype)


def setup_inputs(seed: int = 0) -> dict:
    key_list = jax.random.split(jax.random.key(seed), 9)
    return {
        "fractions": jnp.clip(0.05 + 0.95 * jax.random.uniform(key_list[0], (G, NZT, NBLK, BLK), jnp.float32) ** block_scale(key_list[0], (G, NZT, NBLK, BLK), ((0, 2), (1, 128)), -0.2, 0.2), 0.05, 1.0),
        "courant": draw_courant(jax.random.fold_in(key_list[8], 71), 0),
        "spread": jnp.clip(jnp.exp(jax.random.uniform(key_list[2], (G,), jnp.float32, math.log(0.05), math.log(0.25))), 0.05, 0.25),
        "inlet_frac": jnp.clip(jax.random.uniform(key_list[3], (G,), jnp.float32, 0.2, 1.0), 0.2, 1.0),
        "flags": plant(jax.random.randint(key_list[4], (NZT, NBLK, BLK), 0, 8), jax.random.fold_in(key_list[4], 1), 0, 7).astype(jnp.int32),
        "table_index": plant(jax.random.randint(key_list[5], (NZT, NBLK), 0, NTAB), jax.random.fold_in(key_list[5], 1), 0, NTAB - 1).astype(jnp.int32),
        "lin_table": noise(key_list[6], (NTAB, G, G), 0.25, 1.5, jnp.float32),
        "quad_table": noise(key_list[7], (NTAB, G, G), 0.15, 0.9, jnp.float32),
    }


def advect(field, courant, spread, inlet_frac, flags):
    ext = jnp.pad(field, ((0, 0), (2, 2), (0, 0), (0, 0)))
    lower2 = ext[:, :-4]
    lower1 = ext[:, 1:-3]
    centre = ext[:, 2:-2]
    upper1 = ext[:, 3:-1]
    upper2 = ext[:, 4:]
    pos = jnp.maximum(courant, 0.0)[:, None, None, None]
    neg = jnp.minimum(courant, 0.0)[:, None, None, None]
    disp = spread[:, None, None, None]
    moved = centre - pos * 0.5 * (3.0 * centre - 4.0 * lower1 + lower2)
    moved = moved + pos * pos * 0.5 * (centre - 2.0 * lower1 + lower2)
    moved = moved - neg * 0.5 * (-3.0 * centre + 4.0 * upper1 - upper2)
    moved = moved + neg * neg * 0.5 * (centre - 2.0 * upper1 + upper2)
    moved = moved + disp * (upper1 - 2.0 * centre + lower1)
    moved = jnp.where(flags[None] == 2, jnp.float32(0.0), moved)
    moved = jnp.where(flags[None] == 1, inlet_frac[:, None, None, None] * jnp.ones_like(moved), moved)
    return moved


def regroup(blocks, table_index, lin_table, quad_table):
    lin = lin_table[table_index]
    quad = quad_table[table_index]
    lin_part = jnp.einsum("zbij,jzbc->izbc", lin, blocks, precision=lax.Precision.HIGHEST)
    quad_part = jnp.einsum("zbij,jzbc->izbc", quad, blocks, precision=lax.Precision.HIGHEST)
    return blocks + 0.25 * (lin_part + blocks * quad_part)


def reference(fractions, courant, spread, inlet_frac, flags, table_index, lin_table, quad_table):
    first = advect(fractions, courant, spread, inlet_frac, flags)
    second = regroup(first, table_index, lin_table, quad_table)
    third = advect(second, courant, spread, inlet_frac, flags)
    return regroup(third, table_index, lin_table, quad_table)
```

```python
import functools

import jax
import jax.numpy as jnp
from jax import lax
from jax.experimental import pallas as pl
from jax.experimental.pallas import tpu as pltpu
from jax.sharding import PartitionSpec as P

CHUNKS = 2
SUB = 8
F32 = jnp.float32
BF16 = jnp.bfloat16


def setup(me, courant, spread, inlet, perm, coef, groups):
    half = groups // 2
    quarter = half // 2
    for role in range(2):
        base = jnp.where(me == role, 0, half)
        npos = jnp.int32(0)
        nneg = jnp.int32(0)
        for g in range(half):
            c = courant[base + g]
            pos = c > 0.0
            slot = jnp.where(pos, role * quarter + npos, half + role * quarter + nneg)
            npos = npos + jnp.where(pos, 1, 0)
            nneg = nneg + jnp.where(pos, 0, 1)
            perm[slot] = role * half + g
            if coef is not None:
                a = jnp.where(pos, c, -c)
                s = spread[base + g]
                coef[0, slot] = 1.0 - 1.5 * a + 0.5 * a * a - 2.0 * s
                coef[1, slot] = 2.0 * a - a * a + s
                coef[2, slot] = 0.5 * a * a - 0.5 * a
                coef[3, slot] = s
                coef[4, slot] = inlet[base + g]


def pack_halo(load, perm, up, down, groups, planes):
    half = groups // 2
    for i in range(half):
        p = perm[i]
        up[2 * i] = load(i, p, planes - 2)
        up[2 * i + 1] = load(i, p, planes - 1)
        down[groups + i] = load(i, p, 0)
        n = perm[half + i]
        up[groups + i] = load(i, n, planes - 1)
        down[2 * i] = load(i, n, 0)
        down[2 * i + 1] = load(i, n, 1)


def halo_kernel(me, courant, own, peer, up, down, perm):
    planes = own.shape[1]
    groups = 2 * own.shape[0]
    half = groups // 2
    quarter = half // 2

    @pl.when(pl.program_id(0) == 0)
    def _():
        setup(me[0], courant, None, None, perm, None, groups)

    def load(i, row, z):
        if i < quarter:
            return own[row, z]
        return peer[row - half, z]

    pack_halo(load, perm, up, down, groups, planes)


def step_kernel(
    chunk, last, me, courant, spread, inlet, tidx, *refs
):
    if last:
        src, low, high, flags, tab, _, keep, send, perm, coef, scr, res = refs
        groups = src.shape[0]
        planes = src.shape[1]
    else:
        own, peer, low, high, flags, tab, second, up, down, perm, coef, scr, res = refs
        groups = 2 * own.shape[0]
        planes = own.shape[1]
    half = groups // 2
    quarter = half // 2
    step = pl.program_id(0)
    rows = planes * SUB

    @pl.when(step == 0)
    def _():
        setup(me[0], courant, spread, inlet, perm, coef, groups)

    wall = [flags[z] == 2 for z in range(planes)]
    entry = [flags[z] == 1 for z in range(planes)]
    for i in range(groups):
        row = perm[i]
        if last:
            f = [src[row, z] for z in range(planes)]
        elif i % half < quarter:
            f = [own[row, z] for z in range(planes)]
        else:
            f = [peer[row - half, z] for z in range(planes)]
        c0, c1, c2, c3, c4 = (coef[k, i] for k in range(5))
        if i < half:
            ext = [low[2 * i], low[2 * i + 1]] + f + [high[groups + i]]
            taps = [(ext[z + 2], ext[z + 1], ext[z], ext[z + 3]) for z in range(planes)]
        else:
            k = i - half
            ext = [low[groups + k]] + f + [high[2 * k], high[2 * k + 1]]
            taps = [(ext[z + 1], ext[z + 2], ext[z + 3], ext[z]) for z in range(planes)]
        for z in range(planes):
            a, b, c, d = taps[z]
            v = (c0 * a + c1 * b) + (c2 * c + c3 * d)
            v = jnp.where(wall[z], 0.0, v)
            v = jnp.where(entry[z], c4, v)
            scr[pl.ds(row * rows + z * SUB, SUB), :] = v

    first_block = me[1] + chunk + step * SUB
    for z in range(planes):
        for b in range(SUB):
            r = z * SUB + b
            x = scr[pl.ds(r, groups, stride=rows), :]
            hi = x.astype(BF16)
            lo = (x - hi.astype(F32)).astype(BF16)
            rhs = jnp.concatenate([hi, hi, lo], axis=0)
            t = tidx[z, first_block + b]
            y = jnp.dot(tab[t], rhs, preferred_element_type=F32)
            out = x + (y[:groups] + x * y[groups:])
            res[pl.ds(r, groups, stride=rows), :] = out

    def done(g, z):
        return res[pl.ds(g * rows + z * SUB, SUB), :]

    if last:
        for g in range(half):
            for z in range(planes):
                keep[g, z] = done(g, z)
                send[g, z] = done(half + g, z)
    else:
        for g in range(groups):
            for z in range(planes):
                second[g, z] = done(g, z)
        pack_halo(lambda i, row, z: done(row, z), perm, up, down, groups, planes)


def smem():
    return pl.BlockSpec(memory_space=pltpu.SMEM)


def body(fractions, courant, spread, inlet_frac, flags, table_index, lin_table, quad_table):
    half, planes, nblk, width = fractions.shape
    groups = 2 * half
    ntab = lin_table.shape[0]
    member = lax.axis_index("ga")
    mine = nblk // 2
    size = mine // CHUNKS
    steps = size // SUB
    nhalo = 3 * half
    count = lax.axis_size("gz")
    forward = [(i, i + 1) for i in range(count - 1)]
    backward = [(b, a) for a, b in forward]
    swap = [(0, 1), (1, 0)]
    own_base = member * mine
    peer_base = (1 - member) * mine
    me = jnp.stack([member, own_base, own_base // SUB, peer_base // SUB]).astype(jnp.int32)

    def tables():
        both = jnp.concatenate([lin_table, quad_table], axis=1) * 0.25
        swapped = jnp.concatenate([both[:, :, half:], both[:, :, :half]], axis=2)
        swapped = jnp.concatenate(
            [swapped[:, half:groups], swapped[:, :half], swapped[:, groups + half:], swapped[:, groups:groups + half]],
            axis=1,
        )
        both = jnp.where(member == 1, swapped, both)
        hi = lax.reduce_precision(both, 8, 7)
        lo = both - hi
        return jnp.concatenate([hi, lo, hi], axis=2).astype(BF16)

    def spec(lead, at=None):
        n = len(lead)

        def index(i, me_ref, c=at):
            return (0,) * n + ((i if c is None else me_ref[2] + c + i), 0)

        return pl.BlockSpec(tuple(lead) + (SUB, width), index)

    def shape(*dims):
        return jax.ShapeDtypeStruct(dims, F32)

    def call(kernel, ins, outs, in_specs, out_specs, scratch, aliases={}, flops=0):
        nbytes = sum(x.size * 4 for x in outs) * 2
        return pl.pallas_call(
            kernel,
            out_shape=outs,
            grid_spec=pltpu.PrefetchScalarGridSpec(
                num_scalar_prefetch=1,
                grid=(steps,),
                in_specs=in_specs,
                out_specs=out_specs,
                scratch_shapes=scratch,
            ),
            input_output_aliases=aliases,
            cost_estimate=pl.CostEstimate(flops=flops, bytes_accessed=nbytes, transcendentals=0),
        )(me, *ins)

    sends = []
    for c in range(CHUNKS):
        sends.append(lax.dynamic_slice_in_dim(fractions, peer_base + c * size, size, axis=2))
    got = [lax.ppermute(x, "ga", swap) for x in sends]
    tab = tables()

    tiles = [
        pltpu.SMEM((groups,), jnp.int32),
    ]
    work = [
        pltpu.SMEM((groups,), jnp.int32),
        pltpu.SMEM((5, groups), F32),
        pltpu.VMEM((groups * planes * SUB, width), F32),
        pltpu.VMEM((groups * planes * SUB, width), F32),
    ]
    tab_spec = pl.BlockSpec((ntab, 2 * groups, 3 * groups), lambda i, m: (0, 0, 0))
    flops = 2 * 2 * groups * 3 * groups * planes * size * width

    out = None
    returned = []
    for c in range(CHUNKS):
        at = c * steps
        halo_spec = spec((nhalo,))
        halo_shape = shape(nhalo, size, width)
        up, down = call(
            halo_kernel,
            (courant, fractions, got[c]),
            (halo_shape, halo_shape),
            [smem(), spec((half, planes), at), spec((half, planes))],
            (halo_spec, halo_spec),
            tiles,
        )
        low = lax.ppermute(up, "gz", forward)
        high = lax.ppermute(down, "gz", backward)
        second, up, down = call(
            functools.partial(step_kernel, c * size, False),
            (courant, spread, inlet_frac, table_index, fractions, got[c], low, high, flags, tab),
            (shape(groups, planes, size, width), halo_shape, halo_shape),
            [smem()] * 4
            + [spec((half, planes), at), spec((half, planes)), halo_spec, halo_spec, spec((planes,), at), tab_spec],
            (spec((groups, planes)), halo_spec, halo_spec),
            work,
            flops=flops,
        )
        low = lax.ppermute(up, "gz", forward)
        high = lax.ppermute(down, "gz", backward)
        prior = jnp.zeros((1,), F32) if out is None else out
        out, send = call(
            functools.partial(step_kernel, c * size, True),
            (courant, spread, inlet_frac, table_index, second, low, high, flags, tab, prior),
            (shape(half, planes, nblk, width), shape(half, planes, size, width)),
            [smem()] * 4
            + [spec((groups, planes)), halo_spec, halo_spec, spec((planes,), at), tab_spec, pl.BlockSpec(memory_space=pl.ANY)],
            (spec((half, planes), at), spec((half, planes))),
            work,
            aliases={} if c == 0 else {10: 0},
            flops=flops,
        )
        returned.append(lax.ppermute(send, "ga", swap))

    def place(block, c):
        def copy(m, src, _, dst):
            dst[...] = src[...]

        return pl.pallas_call(
            copy,
            out_shape=shape(half, planes, nblk, width),
            grid_spec=pltpu.PrefetchScalarGridSpec(
                num_scalar_prefetch=1,
                grid=(steps,),
                in_specs=[spec((half, planes)), pl.BlockSpec(memory_space=pl.ANY)],
                out_specs=pl.BlockSpec(
                    (half, planes, SUB, width), lambda i, m: (0, 0, m[3] + c * steps + i, 0)
                ),
            ),
            input_output_aliases={2: 0},
        )(me, block, out)

    for c in range(CHUNKS):
        out = place(returned[c], c)
    return out


def solution(mesh):
    placed = (
        P("ga", "gz", None, None),
        P(),
        P(),
        P(),
        P("gz", None, None),
        P("gz", None),
        P(),
        P(),
    )
    return jax.shard_map(
        body, mesh=mesh, in_specs=placed, out_specs=P("ga", "gz", None, None), check_vma=False
    )
```
